32 devices in a mesh: dp: 4 (over z), ctx: 4 (over x, core), tensor: 2 (over y).
Axes of the slice: x: 2, y: 2, z: 4, core: 2. Of those that a mesh axis runs over, the one named last changes fastest.
Arguments:
- prompt_in: bfloat16 [4, 1024, 2048], P('dp', 'ctx'), may hold values from -6 to 6
- cont_in: bfloat16 [4, 4, 256, 2048], P('dp', 'ctx'), may hold values from -6 to 6
- prompt_len: int32 [4], P('dp'), may hold values from 512 to 1024, as said below
- cont_len: int32 [4, 4], P('dp', 'ctx'), may hold values from 64 to 256, as said below
- ln1_gain: bfloat16 [2048], P(('dp', 'ctx')), may hold values from 0.25 to 1.75
- ln1_bias: bfloat16 [2048], P(('dp', 'ctx')), may hold values from -1.25 to 1.25
- w_query: bfloat16 [2048, 2048], P(('dp', 'ctx'), 'tensor'), may hold values from -0.125 to 0.125
- b_query: bfloat16 [2048], P('tensor'), may hold values from -1.75 to 1.75
- w_kv: bfloat16 [2048, 256], P(('dp', 'ctx'), 'tensor'), may hold values from -0.125 to 0.125
- b_value: bfloat16 [128], P('tensor'), may hold values from -0.1875 to 0.1875
- w_out: bfloat16 [2048, 2048], P('tensor', ('dp', 'ctx')), may hold values from -2 to 2
- b_out: bfloat16 [2048], P(('dp', 'ctx')), may hold values from -1.25 to 1.25
- ln2_gain: bfloat16 [2048], P(('dp', 'ctx')), may hold values from 0.25 to 1.75
- ln2_bias: bfloat16 [2048], P(('dp', 'ctx')), may hold values from -1.25 to 1.25
- w_fc1: bfloat16 [2048, 8192], P(('dp', 'ctx'), 'tensor'), may hold values from -0.125 to 0.125
- b_fc1: bfloat16 [8192], P('tensor'), may hold values from -3 to 3
- w_fc2: bfloat16 [8192, 2048], P('tensor', ('dp', 'ctx')), may hold values from -0.0625 to 0.0625
- b_fc2: bfloat16 [2048], P(('dp', 'ctx')), may hold values from -1.25 to 1.25
- prompt_grad: bfloat16 [4, 1024, 2048], P('dp', 'ctx'), may hold values from -6 to 6
- cont_grad: bfloat16 [4, 4, 256, 2048], P('dp', 'ctx'), may hold values from -6 to 6
Outputs:
- prompt_out: bfloat16 [4, 1024, 2048], P('dp', 'ctx')
- cont_out: bfloat16 [4, 4, 256, 2048], P('dp', 'ctx')
- prompt_dx: bfloat16 [4, 1024, 2048], P('dp', 'ctx')
- cont_dx: bfloat16 [4, 4, 256, 2048], P('dp', 'ctx')
- grad_ln1_gain: float32 [2048], P(('dp', 'ctx'))
- grad_ln1_bias: float32 [2048], P(('dp', 'ctx'))
- grad_w_query: float32 [2048, 2048], P(('dp', 'ctx'), 'tensor')
- grad_b_query: float32 [2048], P('tensor')
- grad_w_kv: float32 [2048, 256], P(('dp', 'ctx'), 'tensor')
- grad_b_value: float32 [128], P('tensor')
- grad_w_out: float32 [2048, 2048], P('tensor', ('dp', 'ctx'))
- grad_b_out: float32 [2048], P(('dp', 'ctx'))
- grad_ln2_gain: float32 [2048], P(('dp', 'ctx'))
- grad_ln2_bias: float32 [2048], P(('dp', 'ctx'))
- grad_w_fc1: float32 [2048, 8192], P(('dp', 'ctx'), 'tensor')
- grad_b_fc1: float32 [8192], P('tensor')
- grad_w_fc2: float32 [8192, 2048], P('tensor', ('dp', 'ctx'))
- grad_b_fc2: float32 [2048], P(('dp', 'ctx'))
The draws below stay inside these ranges and needn't reach their ends.
Inputs may be any that keep to these rules, and one draw needn't show every extreme that they name: Prompt positions from prompt_len on are padding that no query reads as a key. Positions of a continuation from its cont_len on are padding that no query reads as a key.
All inputs are finite; a program needn't handle non-finite values.
Results may differ from the reference program's by a relative error of at most 0.02.
Values may be sent and summed in bfloat16 or wider, within the bound.
No kernel may reach another device: no remote copies, remote signals or barrier semaphores. Data moves between devices by JAX's collectives and lax.ppermute only.
A program may use at most 256 MiB of HBM per device.

```python
import jax
import jax.numpy as jnp
from jax import lax

D = 2048
HEADS = 16
HD = 128
FF = 8192
P_SIZE = 1024
C = 4
L = 256
GROUPS = 4
N_TENSOR = 2


def draw_prompt_len(key, part):
    lengths = jax.random.randint(key, (GROUPS,), P_SIZE // 2, P_SIZE + 1, dtype=jnp.int32)
    return lengths.at[0].set(P_SIZE).at[GROUPS - 1].set(P_SIZE // 2)


def draw_cont_len(key, part):
    lengths = jax.random.randint(key, (GROUPS, C), L // 4, L + 1, dtype=jnp.int32)
    return lengths.at[0, 0].set(L).at[GROUPS - 1, C - 1].set(L // 4)


def level_of(rng, extent, split, low, high):
    def one(dim, shards_of):
        steps = jax.random.uniform(jax.random.fold_in(jax.random.fold_in(rng, 6), dim), (shards_of,), jnp.float32, low / len(split), high / len(split))
        return jnp.repeat(jnp.exp(steps), extent[dim] // shards_of).reshape((-1,) + (1,) * (len(extent) - dim - 1))

    factor_of = one(*split[0])
    for cut in split[1:]:
        factor_of = factor_of * one(*cut)
    return factor_of


def scatter_about(key, dims, width, limit, split=(), kind=jnp.bfloat16):
    array = width * jax.random.normal(key, dims, jnp.float32)
    if split:
        array = array * level_of(key, dims, split, -0.22, 0.18)
    return jnp.clip(array, -limit, limit).astype(kind)


def setup_inputs(seed: int = 0) -> dict:
    key_of = jax.random.split(jax.random.key(seed), 21)
    return {
        "prompt_in": scatter_about(key_of[0], (GROUPS, P_SIZE, D), 1.0, 6.0, ((0, 4), (1, 4))),
        "cont_in": scatter_about(key_of[1], (GROUPS, C, L, D), 1.0, 6.0, ((0, 4), (1, 4))),
        "prompt_len": draw_prompt_len(jax.random.fold_in(key_of[20], 71), 0),
        "cont_len": draw_cont_len(jax.random.fold_in(key_of[20], 71), 0),
        "ln1_gain": jnp.clip(1.0 + 0.15 * jax.random.normal(key_of[4], (D,), jnp.float32), 0.25, 1.75).astype(jnp.bfloat16),
        "ln1_bias": scatter_about(key_of[5], (D,), 0.2, 1.25, ((0, 16),)),
        "w_query": scatter_about(key_of[6], (D, D), D ** -0.5, 0.125, ((0, 16), (1, 2))),
        "b_query": scatter_about(key_of[7], (D,), 0.3, 1.75, ((0, 2),)),
        "w_kv": scatter_about(key_of[8], (D, 2 * HD), D ** -0.5, 0.125, ((0, 16), (1, 2))),
        "b_value": scatter_about(key_of[9], (HD,), 0.03, 0.1875, ((0, 2),)),
        "w_out": scatter_about(key_of[10], (D, D), 8 ** -0.5, 2.0, ((0, 2), (1, 16))),
        "b_out": scatter_about(key_of[11], (D,), 0.2, 1.25, ((0, 16),)),
        "ln2_gain": jnp.clip(1.0 + 0.15 * jax.random.normal(key_of[12], (D,), jnp.float32), 0.25, 1.75).astype(jnp.bfloat16),
        "ln2_bias": scatter_about(key_of[13], (D,), 0.2, 1.25, ((0, 16),)),
        "w_fc1": scatter_about(key_of[14], (D, FF), D ** -0.5, 0.125, ((0, 16), (1, 2))),
        "b_fc1": scatter_about(key_of[15], (FF,), 0.5, 3.0, ((0, 2),)),
        "w_fc2": scatter_about(key_of[16], (FF, D), FF ** -0.5, 0.0625, ((0, 2), (1, 16))),
        "b_fc2": scatter_about(key_of[17], (D,), 0.2, 1.25, ((0, 16),)),
        "prompt_grad": scatter_about(key_of[18], (GROUPS, P_SIZE, D), 1.0, 6.0, ((0, 4), (1, 4))),
        "cont_grad": scatter_about(key_of[19], (GROUPS, C, L, D), 1.0, 6.0, ((0, 4), (1, 4))),
    }


@jax.custom_vjp
def low(v):
    return lax.optimization_barrier(v.astype(jnp.bfloat16)).astype(jnp.float32)

@jax.custom_vjp
def low_back(v):
    return v

def low_keep(v):
    return (low(v), None)

def low_pass(kept, grad):
    return (grad,)

def back_keep(v):
    return (v, None)

def back_low(kept, grad):
    return (low(grad),)
low.defvjp(low_keep, low_pass)
low_back.defvjp(back_keep, back_low)
EPSILON = 1e-05
NEGATIVE = -1e+30
HIGHEST = lax.Precision.HIGHEST

def norm_rows(rows, gain, shift):
    center = rows - lax.optimization_barrier(jnp.mean(rows, axis=-1, keepdims=True))
    spread = lax.optimization_barrier(jnp.mean(center * center, axis=-1, keepdims=True))
    return center * lax.rsqrt(spread + EPSILON) * gain + shift

def softmax_rows(scores):
    row_top = lax.optimization_barrier(jnp.max(scores, axis=-1, keepdims=True))
    row_exp = jnp.exp(scores - row_top)
    return row_exp / lax.optimization_barrier(jnp.sum(row_exp, axis=-1, keepdims=True))

def group_layer(params, prompt_rows, cont_rows, prompt_length, cont_length):
    gain_one, shift_one, w_query, b_query, w_kv, b_value, w_out, b_out, gain_two, shift_two, w_fc1, b_fc1, w_fc2, b_fc2 = params
    heads_group = HEADS // N_TENSOR
    units_group = FF // N_TENSOR
    prompt_count = prompt_rows.shape[0]
    cont_count = cont_rows.shape[0]
    cont_size = cont_rows.shape[1]
    factor = 1.0 / HD ** 0.5
    tokens = jnp.concatenate([prompt_rows, cont_rows.reshape(cont_count * cont_size, D)], axis=0)
    normed = low(norm_rows(tokens, gain_one, shift_one))
    queries = low(low_back(jnp.dot(normed, w_query, precision=HIGHEST) + b_query))
    keyval = jnp.dot(normed, w_kv, precision=HIGHEST) + jnp.concatenate([jnp.zeros_like(b_value), b_value])
    keyval = low(keyval)
    prompt_steps = jnp.arange(prompt_count)
    present = prompt_steps < prompt_length
    mask_prompt = (prompt_steps[None, :] <= prompt_steps[:, None]) & present[None, :]
    cont_steps = jnp.arange(cont_size)
    mask_own = (cont_steps[None, None, :] <= cont_steps[None, :, None]) & (cont_steps[None, None, :] < cont_length[:, None, None])
    mask_cont = jnp.concatenate([jnp.broadcast_to(present[None, None, :], (cont_count, cont_size, prompt_count)), mask_own], axis=-1)
    split_prompt = queries[:prompt_count].reshape(prompt_count, N_TENSOR, heads_group, HD).transpose(1, 0, 2, 3)
    split_cont = queries[prompt_count:].reshape(cont_count, cont_size, N_TENSOR, heads_group, HD).transpose(2, 0, 1, 3, 4)
    split_out = w_out.reshape(N_TENSOR, heads_group * HD, D)

    def head_block(running, pieces):
        query_prompt, query_cont, out_rows = pieces
        shared = low_back(keyval)
        key_prompt = shared[:prompt_count, :HD]
        value_prompt = shared[:prompt_count, HD:]
        key_cont = shared[prompt_count:, :HD].reshape(cont_count, cont_size, HD)
        value_cont = shared[prompt_count:, HD:].reshape(cont_count, cont_size, HD)
        raw_prompt = low_back(jnp.einsum('phd,kd->phk', query_prompt, key_prompt, precision=HIGHEST)) * factor
        prob_prompt = low(softmax_rows(jnp.where(mask_prompt[:, None, :], raw_prompt, NEGATIVE)))
        out_prompt = jnp.einsum('phk,kd->phd', prob_prompt, value_prompt, precision=HIGHEST)
        raw_cont = jnp.concatenate([jnp.einsum('clhd,kd->clhk', query_cont, key_prompt, precision=HIGHEST), jnp.einsum('clhd,cmd->clhm', query_cont, key_cont, precision=HIGHEST)], axis=-1)
        raw_cont = low_back(raw_cont) * factor
        prob_cont = low(softmax_rows(jnp.where(mask_cont[:, :, None, :], raw_cont, NEGATIVE)))
        out_cont = jnp.einsum('clhk,kd->clhd', prob_cont[..., :prompt_count], value_prompt, precision=HIGHEST) + jnp.einsum('clhm,cmd->clhd', prob_cont[..., prompt_count:], value_cont, precision=HIGHEST)
        attended = jnp.concatenate([out_prompt.reshape(prompt_count, heads_group * HD), out_cont.reshape(cont_count * cont_size, heads_group * HD)], axis=0)
        attended = low(low_back(attended))
        return (running + low(jnp.dot(attended, out_rows, precision=HIGHEST)), None)
    zeros_rows = jnp.zeros((tokens.shape[0], D), jnp.float32)
    attn_sum, unused = lax.scan(jax.checkpoint(head_block), zeros_rows, (split_prompt, split_cont, split_out))
    middle = tokens + low_back(attn_sum + b_out)
    normed_two = low(norm_rows(middle, gain_two, shift_two))
    split_up = w_fc1.reshape(D, N_TENSOR, units_group).transpose(1, 0, 2)
    split_bias = b_fc1.reshape(N_TENSOR, units_group)
    split_down = w_fc2.reshape(N_TENSOR, units_group, D)

    def unit_block(running, pieces):
        up_cols, up_bias, down_rows = pieces
        hidden = low_back(jnp.dot(normed_two, up_cols, precision=HIGHEST) + up_bias)
        active = low(jax.nn.gelu(hidden, approximate=True))
        return (running + low(jnp.dot(active, down_rows, precision=HIGHEST)), None)
    mlp_sum, unused_two = lax.scan(jax.checkpoint(unit_block), zeros_rows, (split_up, split_bias, split_down))
    result = middle + mlp_sum + b_fc2
    return (result[:prompt_count], result[prompt_count:].reshape(cont_count, cont_size, D))

def reference(prompt_in, cont_in, prompt_len, cont_len, ln1_gain, ln1_bias, w_query, b_query, w_kv, b_value, w_out, b_out, ln2_gain, ln2_bias, w_fc1, b_fc1, w_fc2, b_fc2, prompt_grad, cont_grad):
    params = tuple((weight.astype(jnp.float32) for weight in (ln1_gain, ln1_bias, w_query, b_query, w_kv, b_value, w_out, b_out, ln2_gain, ln2_bias, w_fc1, b_fc1, w_fc2, b_fc2)))

    def whole(params, prompt_rows, cont_rows):

        def one_group(pieces):
            return group_layer(params, pieces[0], pieces[1], pieces[2], pieces[3])
        return lax.map(jax.checkpoint(one_group), (prompt_rows, cont_rows, prompt_len, cont_len))
    outputs, pullback = jax.vjp(whole, params, prompt_in.astype(jnp.float32), cont_in.astype(jnp.float32))
    gradients, grad_prompt, grad_cont = pullback((prompt_grad.astype(jnp.float32), cont_grad.astype(jnp.float32)))
    return (outputs[0].astype(jnp.bfloat16), outputs[1].astype(jnp.bfloat16), grad_prompt.astype(jnp.bfloat16), grad_cont.astype(jnp.bfloat16), gradients[0], gradients[1], gradients[2], gradients[3], gradients[4], gradients[5], gradients[6], gradients[7], gradients[8], gradients[9], gradients[10], gradients[11], gradients[12], gradients[13])
```

```python
import functools

import jax
import jax.numpy as jnp
from jax import lax
from jax.experimental import pallas as pl
from jax.experimental.pallas import tpu as pltpu
from jax.sharding import PartitionSpec as P

EPSILON = 1e-05
NEGATIVE = -1e30


def norm_rows(rows, gain, shift):
    center = rows - jnp.mean(rows, axis=-1, keepdims=True)
    spread = jnp.mean(center * center, axis=-1, keepdims=True)
    return center * lax.rsqrt(spread + EPSILON) * gain + shift


def gelu_tanh(values):
    return jax.nn.gelu(values, approximate=True)


def product(left, right):
    return jnp.dot(left, right, preferred_element_type=jnp.float32)


def product_inner(left, right):
    return lax.dot_general(
        left, right, (((0,), (0,)), ((), ())), preferred_element_type=jnp.float32
    )


def product_outer(left, right):
    return lax.dot_general(
        left, right, (((1,), (1,)), ((), ())), preferred_element_type=jnp.float32
    )


def build_masks(prompt_len, cont_len, prompt_rows, full_prompt, cont_size):
    offset = lax.axis_index("ctx") * prompt_rows
    query_steps = offset + jnp.arange(prompt_rows, dtype=jnp.int32)
    key_steps = jnp.arange(full_prompt, dtype=jnp.int32)
    present = key_steps[None, :] < prompt_len[:, None]
    mask_prompt = (key_steps[None, None, :] <= query_steps[None, :, None]) & present[:, None, :]
    cont_steps = jnp.arange(cont_size, dtype=jnp.int32)
    mask_own = (cont_steps[None, None, None, :] <= cont_steps[None, None, :, None]) & (
        cont_steps[None, None, None, :] < cont_len[:, :, None, None]
    )
    return (mask_prompt, present, mask_own)


def scores_all(query_prompt, query_cont, prompt_kv, cont_kv, masks, factor):
    head_size = query_prompt.shape[-1]
    mask_prompt, present, mask_own = masks
    key_prompt = prompt_kv[..., :head_size]
    key_cont = cont_kv[..., :head_size]
    score_pp = (
        jnp.einsum("gjhd,gkd->gjhk", query_prompt, key_prompt, preferred_element_type=jnp.float32)
        * factor
    )
    score_pp = jnp.where(mask_prompt[:, :, None, :], score_pp, NEGATIVE)
    score_cp = (
        jnp.einsum("gcjhd,gkd->gcjhk", query_cont, key_prompt, preferred_element_type=jnp.float32)
        * factor
    )
    score_cp = jnp.where(present[:, None, None, None, :], score_cp, NEGATIVE)
    score_co = (
        jnp.einsum("gcjhd,gcmd->gcjhm", query_cont, key_cont, preferred_element_type=jnp.float32)
        * factor
    )
    score_co = jnp.where(mask_own[:, :, :, None, :], score_co, NEGATIVE)
    return (score_pp, score_cp, score_co)


def log_single(scores):
    row_top = jnp.max(scores, axis=-1)
    return row_top + jnp.log(jnp.sum(jnp.exp(scores - row_top[..., None]), axis=-1))


def log_pair(first, second):
    row_top = jnp.maximum(jnp.max(first, axis=-1), jnp.max(second, axis=-1))
    summed = jnp.sum(jnp.exp(first - row_top[..., None]), axis=-1) + jnp.sum(
        jnp.exp(second - row_top[..., None]), axis=-1
    )
    return row_top + jnp.log(summed)


def attend(query_prompt, query_cont, prompt_kv, cont_kv, masks, factor):
    head_size = query_prompt.shape[-1]
    value_prompt = prompt_kv[..., head_size:]
    value_cont = cont_kv[..., head_size:]
    score_pp, score_cp, score_co = scores_all(
        query_prompt, query_cont, prompt_kv, cont_kv, masks, factor
    )
    norm_prompt = log_single(score_pp)
    norm_cont = log_pair(score_cp, score_co)
    weight_pp = jnp.exp(score_pp - norm_prompt[..., None]).astype(jnp.bfloat16)
    out_prompt = jnp.einsum(
        "gjhk,gkd->gjhd", weight_pp, value_prompt, preferred_element_type=jnp.float32
    )
    weight_cp = jnp.exp(score_cp - norm_cont[..., None]).astype(jnp.bfloat16)
    weight_co = jnp.exp(score_co - norm_cont[..., None]).astype(jnp.bfloat16)
    out_cont = jnp.einsum(
        "gcjhk,gkd->gcjhd", weight_cp, value_prompt, preferred_element_type=jnp.float32
    ) + jnp.einsum("gcjhm,gcmd->gcjhd", weight_co, value_cont, preferred_element_type=jnp.float32)
    return (out_prompt, out_cont, norm_prompt, norm_cont)


def attend_back(
    query_prompt,
    query_cont,
    prompt_kv,
    cont_kv,
    masks,
    factor,
    norm_prompt,
    norm_cont,
    back_prompt,
    back_cont,
):
    head_size = query_prompt.shape[-1]
    key_prompt = prompt_kv[..., :head_size]
    value_prompt = prompt_kv[..., head_size:]
    key_cont = cont_kv[..., :head_size]
    value_cont = cont_kv[..., head_size:]
    score_pp, score_cp, score_co = scores_all(
        query_prompt, query_cont, prompt_kv, cont_kv, masks, factor
    )
    weight_pp = jnp.exp(score_pp - norm_prompt[..., None])
    slope_pp = jnp.einsum(
        "gjhd,gkd->gjhk", back_prompt, value_prompt, preferred_element_type=jnp.float32
    )
    delta_prompt = jnp.sum(weight_pp * slope_pp, axis=-1, keepdims=True)
    change_pp = (factor * weight_pp * (slope_pp - delta_prompt)).astype(jnp.bfloat16)
    grad_query_prompt = jnp.einsum(
        "gjhk,gkd->gjhd", change_pp, key_prompt, preferred_element_type=jnp.float32
    )
    grad_key_prompt = jnp.einsum(
        "gjhk,gjhd->gkd", change_pp, query_prompt, preferred_element_type=jnp.float32
    )
    grad_value_prompt = jnp.einsum(
        "gjhk,gjhd->gkd",
        weight_pp.astype(jnp.bfloat16),
        back_prompt,
        preferred_element_type=jnp.float32,
    )
    weight_cp = jnp.exp(score_cp - norm_cont[..., None])
    weight_co = jnp.exp(score_co - norm_cont[..., None])
    slope_cp = jnp.einsum(
        "gcjhd,gkd->gcjhk", back_cont, value_prompt, preferred_element_type=jnp.float32
    )
    slope_co = jnp.einsum(
        "gcjhd,gcmd->gcjhm", back_cont, value_cont, preferred_element_type=jnp.float32
    )
    delta_cont = jnp.sum(weight_cp * slope_cp, axis=-1, keepdims=True) + jnp.sum(
        weight_co * slope_co, axis=-1, keepdims=True
    )
    change_cp = (factor * weight_cp * (slope_cp - delta_cont)).astype(jnp.bfloat16)
    change_co = (factor * weight_co * (slope_co - delta_cont)).astype(jnp.bfloat16)
    grad_query_cont = jnp.einsum(
        "gcjhk,gkd->gcjhd", change_cp, key_prompt, preferred_element_type=jnp.float32
    ) + jnp.einsum("gcjhm,gcmd->gcjhd", change_co, key_cont, preferred_element_type=jnp.float32)
    grad_key_prompt = grad_key_prompt + jnp.einsum(
        "gcjhk,gcjhd->gkd", change_cp, query_cont, preferred_element_type=jnp.float32
    )
    grad_value_prompt = grad_value_prompt + jnp.einsum(
        "gcjhk,gcjhd->gkd",
        weight_cp.astype(jnp.bfloat16),
        back_cont,
        preferred_element_type=jnp.float32,
    )
    grad_key_cont = jnp.einsum(
        "gcjhm,gcjhd->gcmd", change_co, query_cont, preferred_element_type=jnp.float32
    )
    grad_value_cont = jnp.einsum(
        "gcjhm,gcjhd->gcmd",
        weight_co.astype(jnp.bfloat16),
        back_cont,
        preferred_element_type=jnp.float32,
    )
    return (
        grad_query_prompt,
        grad_query_cont,
        jnp.concatenate([grad_key_prompt, grad_value_prompt], axis=-1),
        jnp.concatenate([grad_key_cont, grad_value_cont], axis=-1),
    )


def advance(inputs, params, with_output):
    prompt_in, cont_in, prompt_len, cont_len = inputs
    (
        ln1_gain,
        ln1_bias,
        w_query,
        b_query,
        w_kv,
        b_value,
        w_out,
        b_out,
        ln2_gain,
        ln2_bias,
        w_fc1,
        b_fc1,
        w_fc2,
        b_fc2,
    ) = params
    fetched = (
        lax.all_gather(w_query, ("dp", "ctx"), axis=0, tiled=True),
        lax.all_gather(w_out, ("dp", "ctx"), axis=1, tiled=True),
        lax.all_gather(w_fc1, ("dp", "ctx"), axis=0, tiled=True),
        lax.all_gather(w_fc2, ("dp", "ctx"), axis=1, tiled=True),
        lax.all_gather(w_kv, ("dp", "ctx"), axis=0, tiled=True),
        lax.all_gather(ln1_gain, ("dp", "ctx"), axis=0, tiled=True),
        lax.all_gather(ln1_bias, ("dp", "ctx"), axis=0, tiled=True),
        lax.all_gather(ln2_gain, ("dp", "ctx"), axis=0, tiled=True),
        lax.all_gather(ln2_bias, ("dp", "ctx"), axis=0, tiled=True),
        lax.all_gather(b_out, ("dp", "ctx"), axis=0, tiled=True),
        lax.all_gather(b_fc2, ("dp", "ctx"), axis=0, tiled=True),
    )
    full_query, full_out, full_up, full_down, kv_rows = fetched[:5]
    gain_one, shift_one, gain_two, shift_two, bias_out, bias_down = tuple(
        (piece.astype(jnp.float32) for piece in fetched[5:])
    )
    full_kv, bias_value = (
        lax.all_gather(kv_rows, "tensor", axis=1, tiled=True),
        lax.all_gather(b_value, "tensor", axis=0, tiled=True),
    )
    groups, prompt_rows, width = prompt_in.shape
    conts, cont_size = (cont_in.shape[1], cont_in.shape[2])
    head_size = full_kv.shape[1] // 2
    group_heads = full_query.shape[1] // head_size
    prompt_total = groups * prompt_rows
    cont_total = groups * conts * cont_size
    factor = 1.0 / head_size**0.5
    tokens = jnp.concatenate(
        [prompt_in.reshape(prompt_total, width), cont_in.reshape(cont_total, width)], axis=0
    ).astype(jnp.float32)
    normed = norm_rows(tokens, gain_one, shift_one).astype(jnp.bfloat16)
    queries = (product(normed, full_query) + b_query.astype(jnp.float32)).astype(jnp.bfloat16)
    value_shift = jnp.concatenate(
        [jnp.zeros((head_size,), jnp.float32), bias_value.astype(jnp.float32)]
    )
    keyval = (product(normed, full_kv) + value_shift).astype(jnp.bfloat16)
    prompt_kv = lax.all_gather(
        keyval[:prompt_total].reshape(groups, prompt_rows, 2 * head_size), "ctx", axis=1, tiled=True
    )
    cont_kv = keyval[prompt_total:].reshape(groups, conts, cont_size, 2 * head_size)
    masks = build_masks(prompt_len, cont_len, prompt_rows, prompt_kv.shape[1], cont_size)
    query_prompt = queries[:prompt_total].reshape(groups, prompt_rows, group_heads, head_size)
    query_cont = queries[prompt_total:].reshape(groups, conts, cont_size, group_heads, head_size)
    out_prompt, out_cont, norm_prompt, norm_cont = attend(
        query_prompt, query_cont, prompt_kv, cont_kv, masks, factor
    )
    attended = jnp.concatenate(
        [
            out_prompt.reshape(prompt_total, group_heads * head_size),
            out_cont.reshape(cont_total, group_heads * head_size),
        ],
        axis=0,
    ).astype(jnp.bfloat16)
    branch = lax.psum(product(attended, full_out).astype(jnp.bfloat16), "tensor").astype(
        jnp.float32
    )
    middle = tokens + (branch + bias_out)
    normed_two = norm_rows(middle, gain_two, shift_two).astype(jnp.bfloat16)
    hidden = product(normed_two, full_up) + b_fc1.astype(jnp.float32)
    active = gelu_tanh(hidden).astype(jnp.bfloat16)
    finals = ()
    if with_output:
        feed = lax.psum(product(active, full_down).astype(jnp.bfloat16), "tensor").astype(
            jnp.float32
        )
        result = (middle + feed + bias_down).astype(jnp.bfloat16)
        finals = (
            result[:prompt_total].reshape(prompt_in.shape),
            result[prompt_total:].reshape(cont_in.shape),
        )
    saved = {
        "full_query": full_query,
        "full_out": full_out,
        "full_up": full_up,
        "full_down": full_down,
        "full_kv": full_kv,
        "gain_one": gain_one,
        "shift_one": shift_one,
        "gain_two": gain_two,
        "shift_two": shift_two,
        "tokens": tokens,
        "normed": normed,
        "query_prompt": query_prompt,
        "query_cont": query_cont,
        "prompt_kv": prompt_kv,
        "cont_kv": cont_kv,
        "masks": masks,
        "attended": attended,
        "norm_prompt": norm_prompt,
        "norm_cont": norm_cont,
        "middle": middle,
        "normed_two": normed_two,
        "hidden": hidden,
        "active": active,
    }
    return (saved, finals)


def local(
    prompt_in,
    cont_in,
    prompt_len,
    cont_len,
    ln1_gain,
    ln1_bias,
    w_query,
    b_query,
    w_kv,
    b_value,
    w_out,
    b_out,
    ln2_gain,
    ln2_bias,
    w_fc1,
    b_fc1,
    w_fc2,
    b_fc2,
    prompt_grad,
    cont_grad,
):
    inputs = (prompt_in, cont_in, prompt_len, cont_len)
    params = (
        ln1_gain,
        ln1_bias,
        w_query,
        b_query,
        w_kv,
        b_value,
        w_out,
        b_out,
        ln2_gain,
        ln2_bias,
        w_fc1,
        b_fc1,
        w_fc2,
        b_fc2,
    )
    first, finals = advance(inputs, params, True)
    saved, unused = advance(inputs, params, False)
    groups, prompt_rows, width = prompt_in.shape
    conts, cont_size = (cont_in.shape[1], cont_in.shape[2])
    prompt_total = groups * prompt_rows
    cont_total = groups * conts * cont_size
    head_size = saved["full_kv"].shape[1] // 2
    group_heads = saved["full_query"].shape[1] // head_size
    factor = 1.0 / head_size**0.5
    upstream = jnp.concatenate(
        [prompt_grad.reshape(prompt_total, width), cont_grad.reshape(cont_total, width)], axis=0
    )
    upstream_wide = upstream.astype(jnp.float32)
    grad_down = product_inner(saved["active"], upstream)
    grad_bias_down = jnp.sum(upstream_wide, axis=0)
    back_active = product_outer(upstream, saved["full_down"])
    unused_gelu, gelu_pull = jax.vjp(gelu_tanh, saved["hidden"])
    back_hidden = gelu_pull(back_active)[0].astype(jnp.bfloat16)
    grad_up = product_inner(saved["normed_two"], back_hidden)
    grad_bias_up = jnp.sum(back_hidden.astype(jnp.float32), axis=0)
    back_normed_two = lax.psum(
        product_outer(back_hidden, saved["full_up"]).astype(jnp.bfloat16), "tensor"
    ).astype(jnp.float32)
    unused_norm, norm_pull = jax.vjp(
        norm_rows, saved["middle"], saved["gain_two"], saved["shift_two"]
    )
    back_middle, grad_gain_two, grad_shift_two = norm_pull(back_normed_two)
    back_middle = upstream_wide + back_middle
    back_branch = back_middle.astype(jnp.bfloat16)
    grad_bias_out = jnp.sum(back_branch.astype(jnp.float32), axis=0)
    grad_out = product_inner(saved["attended"], back_branch)
    back_attended = product_outer(back_branch, saved["full_out"]).astype(jnp.bfloat16)
    back_prompt = back_attended[:prompt_total].reshape(groups, prompt_rows, group_heads, head_size)
    back_cont = back_attended[prompt_total:].reshape(
        groups, conts, cont_size, group_heads, head_size
    )
    grad_query_prompt, grad_query_cont, grad_kv_prompt, grad_kv_cont = attend_back(
        saved["query_prompt"],
        saved["query_cont"],
        saved["prompt_kv"],
        saved["cont_kv"],
        saved["masks"],
        factor,
        saved["norm_prompt"],
        saved["norm_cont"],
        back_prompt,
        back_cont,
    )
    grad_kv_owned = lax.psum_scatter(
        grad_kv_prompt.astype(jnp.bfloat16), "ctx", scatter_dimension=1, tiled=True
    ).astype(jnp.float32)
    back_keyval = jnp.concatenate(
        [
            grad_kv_owned.reshape(prompt_total, 2 * head_size),
            grad_kv_cont.reshape(cont_total, 2 * head_size),
        ],
        axis=0,
    ).astype(jnp.bfloat16)
    back_queries = jnp.concatenate(
        [
            grad_query_prompt.reshape(prompt_total, group_heads * head_size),
            grad_query_cont.reshape(cont_total, group_heads * head_size),
        ],
        axis=0,
    ).astype(jnp.bfloat16)
    grad_bias_query = jnp.sum(back_queries.astype(jnp.float32), axis=0)
    grad_query = product_inner(saved["normed"], back_queries)
    grad_kv = product_inner(saved["normed"], back_keyval)
    grad_bias_value = jnp.sum(back_keyval[:, head_size:].astype(jnp.float32), axis=0)
    back_normed = lax.psum(
        (
            product_outer(back_queries, saved["full_query"])
            + product_outer(back_keyval, saved["full_kv"])
        ).astype(jnp.bfloat16),
        "tensor",
    ).astype(jnp.float32)
    unused_first, first_pull = jax.vjp(
        norm_rows, saved["tokens"], saved["gain_one"], saved["shift_one"]
    )
    back_tokens, grad_gain_one, grad_shift_one = first_pull(back_normed)
    back_input = (back_middle + back_tokens).astype(jnp.bfloat16)
    prompt_dx = back_input[:prompt_total].reshape(prompt_in.shape)
    cont_dx = back_input[prompt_total:].reshape(cont_in.shape)
    kv_part, value_part = (
        lax.psum_scatter(
            grad_kv.astype(jnp.bfloat16), "tensor", scatter_dimension=1, tiled=True
        ).astype(jnp.float32),
        lax.psum_scatter(
            grad_bias_value.astype(jnp.bfloat16), "tensor", scatter_dimension=0, tiled=True
        ).astype(jnp.float32),
    )
    spread_count = lax.axis_size(("dp", "ctx"))

    def tiled(vector):
        return jnp.broadcast_to(vector[None, :], (spread_count, vector.shape[0]))

    reduced = (
        lax.psum_scatter(
            grad_query.astype(jnp.bfloat16), ("dp", "ctx"), scatter_dimension=0, tiled=True
        ).astype(jnp.float32),
        lax.psum_scatter(
            grad_out.astype(jnp.bfloat16), ("dp", "ctx"), scatter_dimension=1, tiled=True
        ).astype(jnp.float32),
        lax.psum_scatter(
            grad_up.astype(jnp.bfloat16), ("dp", "ctx"), scatter_dimension=0, tiled=True
        ).astype(jnp.float32),
        lax.psum_scatter(
            grad_down.astype(jnp.bfloat16), ("dp", "ctx"), scatter_dimension=1, tiled=True
        ).astype(jnp.float32),
        lax.psum_scatter(
            kv_part.astype(jnp.bfloat16), ("dp", "ctx"), scatter_dimension=0, tiled=True
        ).astype(jnp.float32),
        lax.psum_scatter(
            grad_gain_one.astype(jnp.bfloat16), ("dp", "ctx"), scatter_dimension=0, tiled=True
        ).astype(jnp.float32),
        lax.psum_scatter(
            grad_shift_one.astype(jnp.bfloat16), ("dp", "ctx"), scatter_dimension=0, tiled=True
        ).astype(jnp.float32),
        lax.psum_scatter(
            grad_gain_two.astype(jnp.bfloat16), ("dp", "ctx"), scatter_dimension=0, tiled=True
        ).astype(jnp.float32),
        lax.psum_scatter(
            grad_shift_two.astype(jnp.bfloat16), ("dp", "ctx"), scatter_dimension=0, tiled=True
        ).astype(jnp.float32),
        lax.psum_scatter(
            grad_bias_out.astype(jnp.bfloat16), ("dp", "ctx"), scatter_dimension=0, tiled=True
        ).astype(jnp.float32),
        lax.psum_scatter(
            grad_bias_down.astype(jnp.bfloat16), ("dp", "ctx"), scatter_dimension=0, tiled=True
        ).astype(jnp.float32),
        lax.psum_scatter(
            tiled(grad_bias_query).astype(jnp.bfloat16),
            ("dp", "ctx"),
            scatter_dimension=0,
            tiled=True,
        ).astype(jnp.float32),
        lax.psum_scatter(
            tiled(grad_bias_up).astype(jnp.bfloat16), ("dp", "ctx"), scatter_dimension=0, tiled=True
        ).astype(jnp.float32),
        lax.psum_scatter(
            tiled(value_part).astype(jnp.bfloat16), ("dp", "ctx"), scatter_dimension=0, tiled=True
        ).astype(jnp.float32),
    )
    return (
        finals[0],
        finals[1],
        prompt_dx,
        cont_dx,
        reduced[5],
        reduced[6],
        reduced[0],
        reduced[11].reshape(-1),
        reduced[4],
        reduced[13].reshape(-1),
        reduced[1],
        reduced[9],
        reduced[7],
        reduced[8],
        reduced[2],
        reduced[12].reshape(-1),
        reduced[3],
        reduced[10],
    )


SIDE = 1
CORE = 2
ACROSS = 4


def block_start(me_ref, index, half, parts, half_rows):
    apart = jnp.bitwise_xor(index % parts, me_ref[0])
    side = jnp.bitwise_xor(index // parts, me_ref[1])
    across = apart // 2
    core = apart % 2
    slot = side * 4 + across if half == 0 else 2 + across * 4 + side
    return pl.multiple_of((core * 8 + slot) * half_rows, half_rows)


def load_keys(starts, qkv_ref, key_s, value_s, width, size, half_rows):
    for number, start in enumerate(starts):
        low = number * half_rows
        key_s[low : low + half_rows, :] = qkv_ref[pl.ds(start, half_rows), width : width + size]
        value_s[low : low + half_rows, :] = qkv_ref[
            pl.ds(start, half_rows), width + size : width + 2 * size
        ]


def stacked(ref, start, heads, size, half_rows):
    return jnp.concatenate(
        [ref[pl.ds(start, half_rows), h * size : (h + 1) * size] for h in range(heads)], axis=0
    )


def block_scores(me_ref, number, query, key_s, half_rows, parts, factor):
    prompt_live = me_ref[2]
    prompt_halves = 2 * parts
    if number < prompt_halves:
        spans = [(0, (number + 1) * half_rows)]
    else:
        first = number - number % 2
        spans = [
            (0, prompt_halves * half_rows),
            (first * half_rows, (number + 1) * half_rows),
        ]
    scores = []
    for which, (low, high) in enumerate(spans):
        raw = (
            lax.dot_general(
                query,
                key_s[low:high, :],
                (((1,), (1,)), ((), ())),
                preferred_element_type=jnp.float32,
            )
            * factor
        )
        column = lax.broadcasted_iota(jnp.int32, raw.shape, 1)
        step = jnp.bitwise_and(lax.broadcasted_iota(jnp.int32, raw.shape, 0), half_rows - 1)
        if number < prompt_halves:
            keep = (column <= step + number * half_rows) & (column < prompt_live)
        elif which == 0:
            keep = column < prompt_live
        else:
            keep = (column <= step + (number % 2) * half_rows) & (
                column < me_ref[3 + (number - prompt_halves) // 2]
            )
        scores.append(jnp.where(keep, raw, NEGATIVE))
    return scores, spans


def attend_kernel(heads, half_rows, size, parts, me_ref, qkv_ref, out_ref, lse_ref, key_s, value_s):
    factor = 1.0 / size**0.5
    width = heads * size
    starts = [
        block_start(me_ref, number // 2, number % 2, parts, half_rows)
        for number in range(4 * parts)
    ]
    load_keys(starts, qkv_ref, key_s, value_s, width, size, half_rows)
    for number, start in enumerate(starts):
        query = stacked(qkv_ref, start, heads, size, half_rows)
        scores, spans = block_scores(me_ref, number, query, key_s, half_rows, parts, factor)
        top = jnp.max(scores[0], axis=-1, keepdims=True)
        for piece in scores[1:]:
            top = jnp.maximum(top, jnp.max(piece, axis=-1, keepdims=True))
        powers = [jnp.exp(piece - top) for piece in scores]
        total = sum(jnp.sum(piece, axis=-1, keepdims=True) for piece in powers)
        scale = 1.0 / total
        mixed = sum(
            jnp.dot(
                (piece * scale).astype(jnp.bfloat16),
                value_s[low:high, :],
                preferred_element_type=jnp.float32,
            )
            for piece, (low, high) in zip(powers, spans)
        ).astype(jnp.bfloat16)
        lse = top + jnp.log(total)
        for head in range(heads):
            rows = slice(head * half_rows, (head + 1) * half_rows)
            out_ref[pl.ds(start, half_rows), head * size : (head + 1) * size] = mixed[rows]
            lse_ref[pl.ds(start, half_rows), head : head + 1] = lse[rows]


def attend_back_kernel(
    heads,
    half_rows,
    size,
    parts,
    me_ref,
    qkv_ref,
    back_ref,
    lse_ref,
    out_ref,
    key_s,
    value_s,
    grad_key_s,
    grad_value_s,
):
    factor = 1.0 / size**0.5
    width = heads * size
    starts = [
        block_start(me_ref, number // 2, number % 2, parts, half_rows)
        for number in range(4 * parts)
    ]
    load_keys(starts, qkv_ref, key_s, value_s, width, size, half_rows)
    grad_key_s[...] = jnp.zeros_like(grad_key_s)
    grad_value_s[...] = jnp.zeros_like(grad_value_s)
    for number, start in enumerate(starts):
        query = stacked(qkv_ref, start, heads, size, half_rows)
        back = stacked(back_ref, start, heads, size, half_rows)
        lse = jnp.concatenate(
            [lse_ref[pl.ds(start, half_rows), h : h + 1] for h in range(heads)], axis=0
        )
        scores, spans = block_scores(me_ref, number, query, key_s, half_rows, parts, factor)
        probs = [jnp.exp(piece - lse) for piece in scores]
        slopes = [
            lax.dot_general(
                back,
                value_s[low:high, :],
                (((1,), (1,)), ((), ())),
                preferred_element_type=jnp.float32,
            )
            for low, high in spans
        ]
        delta = sum(
            jnp.sum(prob * slope, axis=-1, keepdims=True) for prob, slope in zip(probs, slopes)
        )
        grad_query = 0.0
        for prob, slope, (low, high) in zip(probs, slopes, spans):
            change = (factor * prob * (slope - delta)).astype(jnp.bfloat16)
            grad_query = grad_query + jnp.dot(
                change, key_s[low:high, :], preferred_element_type=jnp.float32
            )
            grad_key_s[low:high, :] += lax.dot_general(
                change, query, (((0,), (0,)), ((), ())), preferred_element_type=jnp.float32
            )
            grad_value_s[low:high, :] += lax.dot_general(
                prob.astype(jnp.bfloat16),
                back,
                (((0,), (0,)), ((), ())),
                preferred_element_type=jnp.float32,
            )
        grad_query = grad_query.astype(jnp.bfloat16)
        for head in range(heads):
            out_ref[pl.ds(start, half_rows), head * size : (head + 1) * size] = grad_query[
                head * half_rows : (head + 1) * half_rows
            ]
    for number, start in enumerate(starts):
        rows = slice(number * half_rows, (number + 1) * half_rows)
        out_ref[pl.ds(start, half_rows), width : width + size] = grad_key_s[rows, :].astype(
            jnp.bfloat16
        )
        out_ref[pl.ds(start, half_rows), width + size : width + 2 * size] = grad_value_s[
            rows, :
        ].astype(jnp.bfloat16)


def attend_call(scalars, qkv, heads, half_rows, size, parts):
    total = qkv.shape[0]
    return pl.pallas_call(
        functools.partial(attend_kernel, heads, half_rows, size, parts),
        out_shape=(
            jax.ShapeDtypeStruct((total, heads * size), jnp.bfloat16),
            jax.ShapeDtypeStruct((total, heads), jnp.float32),
        ),
        in_specs=[
            pl.BlockSpec(memory_space=pltpu.SMEM),
            pl.BlockSpec(memory_space=pltpu.VMEM),
        ],
        out_specs=(
            pl.BlockSpec(memory_space=pltpu.VMEM),
            pl.BlockSpec(memory_space=pltpu.VMEM),
        ),
        scratch_shapes=[
            pltpu.VMEM((total, size), jnp.bfloat16),
            pltpu.VMEM((total, size), jnp.bfloat16),
        ],
        compiler_params=pltpu.CompilerParams(vmem_limit_bytes=32 << 20),
        name="attend",
    )(scalars, qkv)


def attend_back_call(scalars, qkv, back, lse, heads, half_rows, size, parts):
    total = qkv.shape[0]
    return pl.pallas_call(
        functools.partial(attend_back_kernel, heads, half_rows, size, parts),
        out_shape=jax.ShapeDtypeStruct((total, (heads + 2) * size), jnp.bfloat16),
        in_specs=[pl.BlockSpec(memory_space=pltpu.SMEM)]
        + [pl.BlockSpec(memory_space=pltpu.VMEM)] * 3,
        out_specs=pl.BlockSpec(memory_space=pltpu.VMEM),
        scratch_shapes=[
            pltpu.VMEM((total, size), jnp.bfloat16),
            pltpu.VMEM((total, size), jnp.bfloat16),
            pltpu.VMEM((total, size), jnp.float32),
            pltpu.VMEM((total, size), jnp.float32),
        ],
        compiler_params=pltpu.CompilerParams(vmem_limit_bytes=32 << 20),
        name="attend_back",
    )(scalars, qkv, back, lse)


def norm_kernel(half_rows, strip, gain_ref, shift_ref, *refs):
    pieces, out_ref = refs[:8], refs[8]
    order = ((0, 0), (2, 0), (0, 1), (1, 1), (1, 0), (3, 0), (2, 1), (3, 1))
    gain = gain_ref[...]
    shift = shift_ref[...]
    for core in range(2):
        for slot, (piece, half) in enumerate(order):
            source = pieces[core * 4 + piece]

            def body(step, carry, source=source, half=half, core=core, slot=slot):
                start = pl.multiple_of(step * strip, strip)
                rows = source[pl.ds(half * half_rows + start, strip), :].astype(jnp.float32)
                center = rows - jnp.mean(rows, axis=-1, keepdims=True)
                spread = jnp.mean(center * center, axis=-1, keepdims=True)
                normed = center * lax.rsqrt(spread + EPSILON) * gain + shift
                out_ref[pl.ds((core * 8 + slot) * half_rows + start, strip), :] = normed.astype(
                    jnp.bfloat16
                )
                return carry

            lax.fori_loop(0, half_rows // strip, body, 0)


def norm_call(pieces, gain, shift):
    rows, width = pieces[0].shape
    half_rows = rows // 2
    return pl.pallas_call(
        functools.partial(norm_kernel, half_rows, 64),
        out_shape=jax.ShapeDtypeStruct((8 * rows, width), jnp.bfloat16),
        in_specs=[pl.BlockSpec(memory_space=pltpu.VMEM)] * 10,
        out_specs=pl.BlockSpec(memory_space=pltpu.VMEM),
        compiler_params=pltpu.CompilerParams(vmem_limit_bytes=40 << 20),
        name="norm_rows",
    )(gain.reshape(1, width), shift.reshape(1, width), *pieces)


def after(value, *first):
    return lax.optimization_barrier((value, *first))[0]


def trade(array, offset):
    size = lax.axis_size(("ctx", "tensor"))
    return lax.ppermute(array, ("ctx", "tensor"), [(i, i ^ offset) for i in range(size)])


def exchange(array, split, join):
    return lax.all_to_all(array, "ctx", split, join, tiled=True)


def with_core(pieces):
    mine = jnp.concatenate(pieces, axis=0)
    theirs = jnp.concatenate([trade(piece, CORE) for piece in pieces], axis=0)
    return jnp.concatenate([mine, theirs], axis=0)


def slab_gather(own, *hold):
    half = own.shape[0] // 2
    top, low = own[:half], own[half:]
    own_core = trade(own, CORE)
    top_across = trade(top, ACROSS)
    low_side = trade(low, SIDE)
    low_across = trade(low, ACROSS)
    top_side = trade(top, SIDE)
    if hold:
        low_across = after(low_across, *hold)
    top_both = trade(top_across, SIDE)
    low_both = trade(low_side, ACROSS)
    pieces = [top_across, low_side, top_side, low_across, top_both, low_both]
    theirs = [trade(piece, CORE) for piece in pieces]

    def arrange(own, pieces):
        top_across, low_side, top_side, low_across, top_both, low_both = pieces
        return [
            own[:half],
            top_across,
            own[half:],
            low_side,
            top_side,
            top_both,
            low_across,
            low_both,
        ]

    return jnp.concatenate(arrange(own, pieces) + arrange(own_core, theirs), axis=0)


def slab_gather_pair(near, far, hold):
    half = near.shape[0] // 2
    near_core, far_core = trade(near, CORE), trade(far, CORE)
    top_across = after(trade(near[:half], ACROSS), hold)
    low_across = after(trade(near[half:], ACROSS), hold)
    top_both = trade(top_across, SIDE)
    low_both = trade(low_across, SIDE)
    pieces = [top_across, low_across, top_both, low_both]
    theirs = [trade(piece, CORE) for piece in pieces]

    def arrange(near, far, pieces):
        top_across, low_across, top_both, low_both = pieces
        return [
            near[:half],
            top_across,
            near[half:],
            far[half:],
            far[:half],
            top_both,
            low_across,
            low_both,
        ]

    return jnp.concatenate(
        arrange(near, far, pieces) + arrange(near_core, far_core, theirs), axis=0
    )


def slab_layout(near, far, near_across, far_across):
    half = near.shape[0] // 2
    return jnp.concatenate(
        [
            near[:half],
            near_across[:half],
            near[half:],
            far[half:],
            far[:half],
            far_across[:half],
            near_across[half:],
            far_across[half:],
        ],
        axis=0,
    )


def widen(array):
    return array.astype(jnp.float32)


def narrow(array):
    return array.astype(jnp.bfloat16)


def reduce_first(multiply, left):
    eighth = left.shape[0] // 8

    def rows(low, high):
        return left[low * eighth : high * eighth]

    far_high = trade(narrow(multiply(rows(6, 8))), CORE)
    far_low = trade(narrow(multiply(rows(4, 6))), CORE)
    top_high = narrow(multiply(rows(2, 3)) + widen(far_high[:eighth]))
    low_high = narrow(multiply(rows(3, 4)) + widen(far_high[eighth:]))
    sent = (top_high, low_high)
    own = after(left[: 2 * eighth], *sent)
    top_low = multiply(own[:eighth]) + widen(far_low[:eighth])
    low_low = multiply(own[eighth:]) + widen(far_low[eighth:])
    kept = lax.optimization_barrier((top_low, low_low))
    return sent, kept, (trade(top_high, SIDE), trade(low_high, ACROSS))


def reduce_second(kept, passed, *hold):
    if hold:
        passed = lax.optimization_barrier(tuple(passed) + tuple(hold))[:2]
    half = kept[0].shape[0] // 2
    sent = tuple(narrow(k[half:] + widen(p[half:])) for k, p in zip(kept, passed))
    last = (trade(sent[0], ACROSS), trade(sent[1], SIDE))
    return sent, tuple(k[:half] + widen(p[:half]) for k, p in zip(kept, passed)), last


def reduce_third(kept, last, *hold):
    if hold:
        last = lax.optimization_barrier(tuple(last) + tuple(hold))[:2]
    return jnp.concatenate([k + widen(p) for k, p in zip(kept, last)], axis=0)


def norm_parts(rows):
    center = rows - jnp.mean(rows, axis=-1, keepdims=True)
    spread_of = jnp.mean(center * center, axis=-1, keepdims=True)
    inverse = lax.rsqrt(spread_of + EPSILON)
    return center * inverse, inverse


def norm_back(grad, unit, inverse, gain):
    scaled = grad * gain
    return inverse * (
        scaled
        - jnp.mean(scaled, axis=-1, keepdims=True)
        - unit * jnp.mean(scaled * unit, axis=-1, keepdims=True)
    )


def sharded(
    prompt_in,
    cont_in,
    prompt_len,
    cont_len,
    ln1_gain,
    ln1_bias,
    w_query,
    b_query,
    w_kv,
    b_value,
    w_out,
    b_out,
    ln2_gain,
    ln2_bias,
    w_fc1,
    b_fc1,
    w_fc2,
    b_fc2,
    prompt_grad,
    cont_grad,
):
    side = lax.axis_index("tensor")
    place = lax.axis_index("ctx")
    slab = lax.axis_index("dp")
    across, core = place // 2, place % 2
    slabs = lax.axis_size("dp")
    parts = lax.axis_size("ctx")
    sides = lax.axis_size("tensor")
    rows, width = prompt_in.shape[1:]
    half_rows = rows // 2
    chunk = ln1_gain.shape[0]
    size = w_kv.shape[1] * sides // 2
    heads = w_query.shape[1] // (size * parts)
    units = w_fc1.shape[1] // parts
    columns = (heads + 2) * size

    def pick(first, second):
        return jnp.where(side == 0, first, second)

    def straighten(array, *flags):
        for axis, flag in flags:
            array = jnp.where(flag == 1, jnp.flip(array, axis), array)
        return array

    def query_block(offset):
        start = jnp.bitwise_xor(place, offset // 2) * (heads * size)
        return lax.dynamic_slice_in_dim(w_query, start, heads * size, 1)

    lengths = jnp.zeros((chunk,), jnp.int32)
    lengths = lengths.at[0].set(cont_len[0, 0] // 128).at[1].set(cont_len[0, 0] % 128)
    value_row = jnp.pad(b_value, (0, chunk - b_value.shape[0]))
    small = jnp.stack(
        [
            ln1_gain,
            ln1_bias,
            ln2_gain,
            ln2_bias,
            b_out,
            b_fc2,
            lengths.astype(jnp.bfloat16),
            value_row,
        ]
    )
    small = jnp.pad(small, ((0, 8), (0, 0)))
    beside = jnp.concatenate([w_kv, small], axis=0)
    beside_other = trade(beside, SIDE)
    offsets = (ACROSS, CORE, ACROSS | CORE)
    blocks = [query_block(offset) for offset in offsets]
    traded = [trade(block, offset) for block, offset in zip(blocks, offsets)]
    prompt_own = after(prompt_in.reshape(rows, width), *blocks)
    cont_own = after(cont_in.reshape(rows, width), *blocks)
    near, far = pick(prompt_own, cont_own), pick(cont_own, prompt_own)
    near_across = trade(near, ACROSS)
    far_across = trade(near_across, SIDE)
    out_block = exchange(after(w_out, *blocks), 0, 1)
    up_block = exchange(after(w_fc1, near_across), 1, 0)

    beside = jnp.concatenate([pick(beside, beside_other), pick(beside_other, beside)], axis=1)
    operand = jnp.concatenate([query_block(0)] + traded + [beside], axis=0)
    gathered = lax.all_gather(operand, "dp", axis=0)
    gathered = after(gathered, out_block, up_block)
    query_rows = parts * chunk
    query_full = gathered[:, :query_rows].reshape(slabs, 2, 2, chunk, heads * size)
    query_full = straighten(query_full, (1, core), (2, across))
    query_full = query_full.transpose(0, 2, 1, 3, 4).reshape(width, heads * size)
    rest = gathered[:, query_rows:]
    near_rest = jnp.stack([rest, trade(rest, ACROSS)])
    rest = jnp.stack([near_rest, trade(near_rest, CORE)])
    rest = straighten(rest, (0, core), (1, across))
    kv_full = rest[:, :, :, :chunk].transpose(2, 1, 0, 3, 4).reshape(width, 2 * size)
    small = rest[:, :, :, chunk : chunk + 8].transpose(2, 1, 0, 3, 4)
    small = small.reshape(slabs * parts, 8, sides, chunk)
    full_qkv = jnp.concatenate([query_full, kv_full], axis=1)

    def vector(number):
        return small[:, number, 0].reshape(width).astype(jnp.float32)

    gain_one, shift_one, gain_two, shift_two, bias_out, bias_down = [vector(i) for i in range(6)]
    length_pair = lax.dynamic_slice_in_dim(small[:, 6, 0, :2], slab * parts, parts, 0)
    length_pair = length_pair.astype(jnp.float32).astype(jnp.int32)
    cont_live = length_pair[:, 0] * 128 + length_pair[:, 1]
    bias_value = small[0, 7, :, : b_value.shape[0]].reshape(size)
    scalars = jnp.concatenate([jnp.stack([place, side, prompt_len[0]]), cont_live]).astype(jnp.int32)

    full_out = lax.all_gather(out_block, "dp", axis=1, tiled=True)
    full_up = lax.all_gather(up_block, "dp", axis=0, tiled=True)
    pieces = [near, far, near_across, after(far_across, near_rest)]
    pieces = pieces + [trade(piece, CORE) for piece in pieces]
    bias_query = lax.dynamic_slice_in_dim(b_query, place * heads * size, heads * size, 0)
    bias_up = lax.dynamic_slice_in_dim(b_fc1, place * units, units, 0)

    normed = norm_call(pieces, gain_one, shift_one)
    shift_qkv = jnp.concatenate(
        [
            bias_query.astype(jnp.float32),
            jnp.zeros((size,), jnp.float32),
            bias_value.astype(jnp.float32),
        ]
    )
    qkv = (product(normed, full_qkv) + shift_qkv).astype(jnp.bfloat16)
    down_block = exchange(after(w_fc2, qkv), 0, 1)
    full_down = lax.all_gather(down_block, "dp", axis=1, tiled=True)
    attended, lse = attend_call(scalars, qkv, heads, half_rows, size, parts)
    attended = after(attended, down_block)
    unused, kept, passed = reduce_first(lambda part: product(part, full_out), attended)
    unused, kept, last = reduce_second(kept, passed, full_up)
    branch = reduce_third(kept, last)
    tokens = near.astype(jnp.float32)
    middle = tokens + (branch + bias_out)
    unit_two, inverse_two = norm_parts(middle)
    normed_two = slab_gather((unit_two * gain_two + shift_two).astype(jnp.bfloat16))
    hidden = product(normed_two, full_up) + bias_up.astype(jnp.float32)
    active = gelu_tanh(hidden).astype(jnp.bfloat16)
    prompt_back = after(prompt_grad.reshape(rows, width), normed_two)
    cont_back = cont_grad.reshape(rows, width)
    grad_near, grad_far = pick(prompt_back, cont_back), pick(cont_back, prompt_back)
    upstream = slab_gather_pair(grad_near, grad_far, active)

    def settle(grad, split):
        return lax.psum_scatter(narrow(grad), "dp", scatter_dimension=split, tiled=True)

    upstream = after(upstream, full_down)
    grad_down = narrow(product_inner(active, upstream))
    sum_down = settle(grad_down, 1)
    active_next = after(active, grad_down)
    sent_feed, kept_feed, passed_feed = reduce_first(
        lambda part: product(part, full_down), active_next
    )
    back_active = product_outer(after(upstream, *sent_feed), full_down)
    unused_gelu, gelu_pull = jax.vjp(gelu_tanh, hidden)
    back_hidden = gelu_pull(back_active)[0].astype(jnp.bfloat16)
    grad_bias_up = jnp.sum(back_hidden.astype(jnp.float32), axis=0)
    sent_feed, kept_feed, last_feed = reduce_second(kept_feed, passed_feed, back_hidden)
    sent_two, kept, passed = reduce_first(
        lambda part: product_outer(part, full_up), after(back_hidden, *sent_feed)
    )
    grad_up = narrow(product_inner(normed_two, after(back_hidden, *sent_two)))
    sum_up = settle(grad_up, 0)
    unused, kept, last = reduce_second(kept, passed)
    back_normed_two = reduce_third(kept, last)
    feed = reduce_third(kept_feed, last_feed, *sent_two)
    result = (middle + feed + bias_down).astype(jnp.bfloat16)
    upstream_wide = grad_near.astype(jnp.float32)
    back_middle = upstream_wide + norm_back(back_normed_two, unit_two, inverse_two, gain_two)
    back_branch_own = back_middle.astype(jnp.bfloat16)
    back_branch = slab_gather(back_branch_own, grad_up)
    result_other = trade(after(result, back_branch), SIDE)
    back_attended = product_outer(back_branch, full_out).astype(jnp.bfloat16)
    back_attended = after(back_attended, sum_down)
    back_qkv = attend_back_call(scalars, qkv, back_attended, lse, heads, half_rows, size, parts)
    grad_out = product_inner(attended, after(back_branch, back_attended))
    sum_out = settle(grad_out, 1)
    down_traded = exchange(after(sum_down, back_branch), 1, 0)
    back_qkv = after(back_qkv, result_other, down_traded)
    sent_one, kept, passed = reduce_first(lambda part: product_outer(part, full_qkv), back_qkv)
    back_last = after(back_qkv, *sent_one)
    grad_qkv = product_inner(normed, back_last)
    sent_last, kept, last = reduce_second(kept, passed, sum_up)
    back_normed = reduce_third(kept, last)
    unit_one, inverse_one = norm_parts(tokens)
    back_input = (back_middle + norm_back(back_normed, unit_one, inverse_one, gain_one)).astype(
        jnp.bfloat16
    )
    back_other = trade(back_input, SIDE)

    out_down = down_traded.astype(jnp.float32)
    out_up = exchange(after(sum_up, back_input), 0, 1).astype(jnp.float32)
    out_out = exchange(after(sum_out, back_input), 1, 0).astype(jnp.float32)

    back_sums = jnp.sum(back_last.astype(jnp.float32), axis=0)
    weights_wide = full_qkv.astype(jnp.float32)
    unit_product = (grad_qkv - shift_one[:, None] * back_sums[None, :]) / gain_one[:, None]
    wide = jnp.stack(
        [
            jnp.sum(unit_product * weights_wide, axis=1),
            jnp.sum(back_sums[None, :] * weights_wide, axis=1),
            jnp.sum(back_normed_two * unit_two, axis=0),
            jnp.sum(back_normed_two, axis=0),
            jnp.sum(back_branch_own.astype(jnp.float32), axis=0),
            jnp.sum(upstream_wide, axis=0),
        ]
    )
    count = wide.shape[0]
    wide_rows = -(-count * chunk // columns)
    wide = wide.reshape(count, slabs * parts, chunk).transpose(1, 0, 2)
    wide = jnp.pad(
        wide.reshape(slabs * parts, count * chunk), ((0, 0), (0, wide_rows * columns - count * chunk))
    )
    shared = jnp.concatenate(
        [grad_bias_up, back_sums[: heads * size], back_sums[(heads + 1) * size :]]
    )
    shared_rows = -(-shared.shape[0] // columns)
    shared = jnp.pad(shared, (0, shared_rows * columns - shared.shape[0]))
    extra = jnp.concatenate(
        [
            wide.reshape(slabs * parts, wide_rows, columns),
            jnp.broadcast_to(
                shared.reshape(1, shared_rows, columns), (slabs * parts, shared_rows, columns)
            ),
        ],
        axis=1,
    )
    extra = jnp.pad(extra, ((0, 0), (0, -extra.shape[1] % 8), (0, 0)))
    packed = jnp.concatenate(
        [grad_qkv.reshape(slabs * parts, chunk, columns), extra], axis=1
    ).astype(jnp.bfloat16)
    packed = lax.psum_scatter(packed, "dp", scatter_dimension=0, tiled=True)
    packed = lax.all_to_all(packed, "ctx", 0, 0, tiled=True)
    out_query = (
        packed[:, :chunk, : heads * size]
        .transpose(1, 0, 2)
        .reshape(chunk, parts * heads * size)
        .astype(jnp.float32)
    )
    kv_sum = jnp.sum(packed[:, :chunk, heads * size :].astype(jnp.float32), axis=0)
    extra = packed[:, chunk:].astype(jnp.float32)
    wide = jnp.sum(extra[:, :wide_rows], axis=0).reshape(-1)[: count * chunk].reshape(count, chunk)
    shared = extra[:, wide_rows : wide_rows + shared_rows].reshape(parts, -1)
    up_vec = shared[:, :units].reshape(-1)
    query_vec = shared[:, units : units + heads * size].reshape(-1)
    value_part = jnp.sum(shared[:, units + heads * size : units + (heads + 1) * size], axis=0)
    kv_mine = pick(kv_sum[:, :size], kv_sum[:, size:])
    kv_theirs = pick(kv_sum[:, size:], kv_sum[:, :size])
    value_part = jnp.pad(value_part.reshape(1, size), ((0, 0), (0, chunk - size)))
    theirs = trade(
        jnp.concatenate([kv_theirs, wide, value_part], axis=0).astype(jnp.bfloat16), SIDE
    ).astype(jnp.float32)
    mine = jnp.concatenate([kv_mine, wide, value_part], axis=0)
    mine = mine.astype(jnp.bfloat16).astype(jnp.float32)
    both = mine + theirs
    out_kv = both[:chunk]
    own_wide = both[chunk : chunk + count]
    value_vec = lax.dynamic_slice_in_dim(
        both[chunk + count], side * b_value.shape[0], b_value.shape[0], 0
    )

    def place_back(mine, other):
        return (
            pick(mine, other).reshape(prompt_in.shape),
            pick(other, mine).reshape(cont_in.shape),
        )

    prompt_out, cont_out = place_back(result, result_other)
    prompt_dx, cont_dx = place_back(back_input, back_other)
    return (
        prompt_out,
        cont_out,
        prompt_dx,
        cont_dx,
        own_wide[0],
        own_wide[1],
        out_query,
        query_vec,
        out_kv,
        value_vec,
        out_out,
        own_wide[4],
        own_wide[2],
        own_wide[3],
        out_up,
        up_vec,
        out_down,
        own_wide[5],
    )


def fits(mesh):
    return dict(mesh.shape)["ctx"] == 4 and dict(mesh.shape)["tensor"] == 2


def solution(mesh):
    placed = (
        P("dp", "ctx", None),
        P("dp", "ctx", None, None),
        P("dp"),
        P("dp", "ctx"),
        P(("dp", "ctx")),
        P(("dp", "ctx")),
        P(("dp", "ctx"), "tensor"),
        P("tensor"),
        P(("dp", "ctx"), "tensor"),
        P("tensor"),
        P("tensor", ("dp", "ctx")),
        P(("dp", "ctx")),
        P(("dp", "ctx")),
        P(("dp", "ctx")),
        P(("dp", "ctx"), "tensor"),
        P("tensor"),
        P("tensor", ("dp", "ctx")),
        P(("dp", "ctx")),
        P("dp", "ctx", None),
        P("dp", "ctx", None, None),
    )
    return jax.shard_map(
        sharded if fits(mesh) else local,
        mesh=mesh,
        in_specs=placed,
        out_specs=(
            P("dp", "ctx", None),
            P("dp", "ctx", None, None),
            P("dp", "ctx", None),
            P("dp", "ctx", None, None),
            P(("dp", "ctx")),
            P(("dp", "ctx")),
            P(("dp", "ctx"), "tensor"),
            P("tensor"),
            P(("dp", "ctx"), "tensor"),
            P("tensor"),
            P("tensor", ("dp", "ctx")),
            P(("dp", "ctx")),
            P(("dp", "ctx")),
            P(("dp", "ctx")),
            P(("dp", "ctx"), "tensor"),
            P("tensor"),
            P("tensor", ("dp", "ctx")),
            P(("dp", "ctx")),
        ),
        check_vma=False,
    )
```
